256 devices in a mesh: ctx: 32 (over z, y_hi, core), head: 8 (over x, y_lo).
Axes of the slice: x: 4, y: 4 (y_hi: 2, y_lo: 2; y = y_hi * 2 + y_lo), z: 8, core: 2. Of those that a mesh axis runs over, the one named last changes fastest.
Arguments:
- queries: bfloat16 [20480, 2048], P('ctx', 'head'), may hold values from -8 to 8
- keys: bfloat16 [20480, 2048], P('ctx', 'head'), may hold values from -6 to 6
- values: bfloat16 [20480, 2048], P('ctx', 'head'), may hold values from -6 to 6
- key_weight: bfloat16 [16, 16, 128], P('head'), may hold values from -1.5 to 1.5
- value_weight: bfloat16 [16, 16, 128], P('head'), may hold values from -1.5 to 1.5
Outputs:
- attended: bfloat16 [20480, 2048], P(('ctx', 'head'))
The draws below stay inside these ranges and needn't reach their ends.
All inputs are finite; a program needn't handle non-finite values.
Results may differ from the reference program's by a relative error of at most 0.0061.
Values may be sent and summed in bfloat16 or wider, within the bound.
No kernel may reach another device: no remote copies, remote signals or barrier semaphores. Data moves between devices by JAX's collectives and lax.ppermute only.
A program may use at most 64 MiB of HBM per device.

```python
import math
import jax
import jax.numpy as jnp
from jax import lax

HD = 128
HEADS = 16
BLOCK = 640
COMP = 16
PARTNERS = 5
TOKENS = 20480
N_CTX = 32


def draw_queries(key, part):
    blocks = TOKENS // BLOCK
    shape = (blocks, BLOCK, HEADS, HD)
    drawn = 2.2 * jax.random.truncated_normal(jax.random.fold_in(key, 1), -3.6, 3.6, shape, jnp.float32)
    return drawn.reshape(TOKENS, HEADS * HD).astype(jnp.bfloat16)


def draw_keys(key, part):
    blocks = TOKENS // BLOCK
    shape = (blocks, BLOCK, HEADS, HD)
    drawn = jax.random.truncated_normal(jax.random.fold_in(key, 2), -6.0, 6.0, shape, jnp.float32)
    return drawn.reshape(TOKENS, HEADS * HD).astype(jnp.bfloat16)


def level_of(key, dims, cuts, least, largest):
    factor_of, own = 1.0, jax.random.fold_in(key, 6)
    for axis_at, shards_of in cuts:
        draws = jnp.exp(jax.random.uniform(jax.random.fold_in(own, axis_at), (shards_of,), jnp.float32, least / len(cuts), largest / len(cuts)))
        factor_of = factor_of * jnp.repeat(draws, dims[axis_at] // shards_of).reshape([-1 if axis == axis_at else 1 for axis in range(len(dims))])
    return factor_of


def bell_draw(key, shape, width, reach, cuts=(), held_as=jnp.bfloat16):
    loudness = level_of(key, shape, cuts, -0.22, 0.18) if cuts else 1.0
    entries = jax.random.normal(key, shape, jnp.float32) * width * loudness
    return jnp.minimum(jnp.maximum(entries, -reach), reach).astype(held_as)


def setup_inputs(seed: int = 0) -> dict:
    seeds = jax.random.split(jax.random.key(seed), 6)
    return {
        "queries": draw_queries(jax.random.fold_in(seeds[5], 71), 0),
        "keys": draw_keys(jax.random.fold_in(seeds[5], 71), 0),
        "values": bell_draw(seeds[2], (TOKENS, HEADS * HD), 1.0, 6.0, ((0, 32), (1, 8))),
        "key_weight": bell_draw(seeds[3], (HEADS, COMP, HD), COMP ** -0.5, 1.5, ((0, 8),)),
        "value_weight": bell_draw(seeds[4], (HEADS, COMP, HD), COMP ** -0.5, 1.5, ((0, 8),)),
    }


def fold_rows(values_in, weight):
    grouped = values_in.astype(jnp.float32).reshape(TOKENS // COMP, COMP, HEADS, HD)
    folded = jnp.einsum('gjhd,hjd->ghd', grouped, weight.astype(jnp.float32))
    return folded.astype(jnp.bfloat16)

def head_attention(operands):
    query_rows, key_rows, value_rows = operands
    score_scale = 1.0 / math.sqrt(HD)
    scores = jnp.dot(query_rows.astype(jnp.float32), key_rows.astype(jnp.float32).T, preferred_element_type=jnp.float32) * score_scale
    row_top = lax.optimization_barrier(jnp.max(scores, axis=1, keepdims=True))
    weights = jnp.exp(scores - row_top)
    row_total = lax.optimization_barrier(jnp.sum(weights, axis=1, keepdims=True))
    rounded = lax.optimization_barrier(weights.astype(jnp.bfloat16)).astype(jnp.float32)
    mixed_rows = jnp.dot(rounded, value_rows.astype(jnp.float32), preferred_element_type=jnp.float32)
    return mixed_rows / row_total

def reference(queries, keys, values, key_weight, value_weight):
    folded_keys = fold_rows(keys, key_weight)
    folded_values = fold_rows(values, value_weight)
    query_blocks = queries.reshape(N_CTX, BLOCK, HEADS, HD)
    key_blocks = keys.reshape(N_CTX, BLOCK, HEADS, HD)
    value_blocks = values.reshape(N_CTX, BLOCK, HEADS, HD)

    def one_block(block_index):
        chosen = [block_index] + [jnp.bitwise_xor(block_index, jnp.int32(1 << bit_level)) for bit_level in range(PARTNERS)]
        near_keys = jnp.concatenate([key_blocks[picked] for picked in chosen] + [folded_keys], 0)
        near_values = jnp.concatenate([value_blocks[picked] for picked in chosen] + [folded_values], 0)
        operands = (jnp.transpose(query_blocks[block_index], (1, 0, 2)), jnp.transpose(near_keys, (1, 0, 2)), jnp.transpose(near_values, (1, 0, 2)))
        return lax.map(head_attention, operands)
    mixed_all = lax.map(one_block, jnp.arange(N_CTX, dtype=jnp.int32))
    return jnp.transpose(mixed_all, (0, 2, 1, 3)).reshape(TOKENS, HEADS * HD).astype(jnp.bfloat16)
```

```python
import functools
import math

import jax
import jax.numpy as jnp
from jax import lax
from jax.experimental import pallas as pl
from jax.experimental.pallas import tpu as pltpu
from jax.sharding import PartitionSpec as P


vmem_spec = pl.BlockSpec(memory_space=pltpu.VMEM)


def z_perm(size, target):
    return [(i, target(i // 4) % (size // 4) * 4 + i % 4) for i in range(size)]


def bit_perm(size, bit):
    return [(i, i ^ (1 << bit)) for i in range(size)]


def fold_kernel(keys, values, key_weight, value_weight, folded):
    for side, (rows, weight) in enumerate(((keys, key_weight), (values, value_weight))):
        head_count, group, width = weight.shape
        for head in range(head_count):
            lanes = slice(head * width, (head + 1) * width)
            block = rows[:, lanes].astype(jnp.float32)
            grouped = block.reshape(block.shape[0] // group, group, width)
            summed = jnp.sum(grouped * weight[head].astype(jnp.float32)[None], axis=1)
            folded[side, :, lanes] = summed.astype(folded.dtype)


def fold_rows(keys, values, key_weight, value_weight):
    rows, channels = keys.shape
    group = key_weight.shape[1]
    return pl.pallas_call(
        fold_kernel,
        name="fold_rows",
        out_shape=jax.ShapeDtypeStruct((2, rows // group, channels), keys.dtype),
        in_specs=[vmem_spec] * 4,
        out_specs=vmem_spec,
        compiler_params=pltpu.CompilerParams(vmem_limit_bytes=16 << 20),
        cost_estimate=pl.CostEstimate(flops=4 * rows * channels, bytes_accessed=4 * rows * channels, transcendentals=0),
    )(keys, values, key_weight, value_weight)


def attend_kernel(pieces, first, last, width, *refs):
    queries, rest = refs[0], refs[1:]
    keys, values, rest = rest[:pieces], rest[pieces : 2 * pieces], rest[2 * pieces :]
    if not first:
        top_in, total_in, sum_in, rest = *rest[:3], rest[3:]
    heads = queries.shape[1] // width
    factor = math.log2(math.e) / math.sqrt(width)

    for head in range(heads):
        lanes = slice(head * width, (head + 1) * width)
        query = queries[:, lanes]
        scores = [
            lax.dot_general(query, k[:, lanes], (((1,), (1,)), ((), ())), preferred_element_type=jnp.float32)
            for k in keys
        ]
        top = functools.reduce(jnp.maximum, [jnp.max(s, axis=1, keepdims=True) for s in scores])
        if not first:
            top_before = top_in[:, lanes][:, :1]
            top = jnp.maximum(top, top_before)
        weights = [jnp.exp2((s - top) * factor) for s in scores]
        total = sum(jnp.sum(w, axis=1, keepdims=True) for w in weights)
        summed = sum(
            jnp.dot(w.astype(jnp.bfloat16), v[:, lanes], preferred_element_type=jnp.float32)
            for w, v in zip(weights, values)
        )
        if not first:
            decay = jnp.exp2((top_before - top) * factor)
            total = total + decay * total_in[:, lanes][:, :1]
            summed = summed + decay * sum_in[:, lanes]
        if last:
            rest[0][:, lanes] = (summed * (1.0 / total)).astype(jnp.bfloat16)
        else:
            rest[0][:, lanes] = jnp.broadcast_to(top, summed.shape)
            rest[1][:, lanes] = jnp.broadcast_to(total, summed.shape)
            rest[2][:, lanes] = summed


def attend(carried, queries, pairs, width, last=False):
    rows, channels = queries.shape
    keys, values = [k for k, _ in pairs], [v for _, v in pairs]
    key_count = sum(k.shape[0] for k in keys)
    operands = [queries, *keys, *values, *(carried or ())]
    if last:
        out_shape = jax.ShapeDtypeStruct((rows, channels), jnp.bfloat16)
        out_specs = vmem_spec
    else:
        out_shape = [jax.ShapeDtypeStruct((rows, channels), jnp.float32)] * 3
        out_specs = [vmem_spec] * 3
    return pl.pallas_call(
        functools.partial(attend_kernel, len(pairs), carried is None, last, width),
        name="attend",
        out_shape=out_shape,
        in_specs=[vmem_spec] * len(operands),
        out_specs=out_specs,
        compiler_params=pltpu.CompilerParams(vmem_limit_bytes=16 << 20),
        cost_estimate=pl.CostEstimate(
            flops=8 * rows * key_count * channels,
            bytes_accessed=4 * key_count * channels + 4 * rows * channels,
            transcendentals=rows * key_count * channels // width,
        ),
    )(*operands)


def move(rows, pairs):
    return lax.ppermute(rows, "ctx", pairs)


def body(queries, keys, values, key_weight, value_weight):
    width = key_weight.shape[2]
    size = lax.axis_size("ctx")
    core, y_side, z_one, z_two, z_four = (bit_perm(size, bit) for bit in range(5))
    z_side = z_perm(size, lambda z: z + 2 if z & 2 else z - 2)
    z_odd = z_perm(size, lambda z: z + 1 if z & 1 else z - 1)

    folded = fold_rows(keys, values, key_weight, value_weight)
    for pairs in (z_four, z_side, z_odd, y_side, core):
        folded = jnp.concatenate([folded, move(folded, pairs)], 1)
    two = move(keys, z_two), move(values, z_two)
    one = move(keys, z_one), move(values, z_one)
    twin = move(keys, core), move(values, core)
    side = move(keys, y_side), move(values, y_side)
    four = move(two[0], z_side), move(two[1], z_side)

    stages = (
        ("own", ((keys, values), twin)),
        ("side", (side,)),
        ("two", (two,)),
        ("one", (one,)),
        ("comp", ((folded[0], folded[1]),)),
        ("four", (four,)),
    )
    carried = None
    for name, pairs in stages:
        carried = attend(carried, queries, pairs, width, last=name == "four")
    return lax.all_to_all(carried, "head", split_axis=0, concat_axis=1, tiled=True)


def solution(mesh):
    in_specs = (
        P("ctx", "head"),
        P("ctx", "head"),
        P("ctx", "head"),
        P("head", None, None),
        P("head", None, None),
    )
    out_specs = P(("ctx", "head"), None)

    return jax.shard_map(body, mesh=mesh, in_specs=in_specs, out_specs=out_specs, check_vma=False)
```

```python
import functools
import math

import jax
import jax.numpy as jnp
from jax import lax
from jax.experimental import pallas as pl
from jax.experimental.pallas import tpu as pltpu
from jax.sharding import PartitionSpec as P


vmem_spec = pl.BlockSpec(memory_space=pltpu.VMEM)


def z_perm(size, target):
    return [(i, target(i // 4) % (size // 4) * 4 + i % 4) for i in range(size)]


def bit_perm(size, bit):
    return [(i, i ^ (1 << bit)) for i in range(size)]


def prepare_kernel(keys, values, key_weight, value_weight, lead, key_tail, low_values, high_values, *scratch):
    weights, sems = scratch[:2], scratch[2]
    cut, half = keys.shape[0] - key_tail.shape[0], low_values.shape[0]
    copies = [
        pltpu.make_async_copy(source, target, sems.at[index])
        for index, (source, target) in enumerate(
            (
                (key_weight, weights[0]),
                (value_weight, weights[1]),
                (keys.at[:cut], lead.at[:cut]),
                (keys.at[cut:], key_tail),
                (values.at[:half], low_values),
                (values.at[half:], high_values),
            )
        )
    ]
    for copy in copies:
        copy.start()
    for copy in copies:
        copy.wait()
    row = cut
    for weight, blocks in zip(weights, ((lead.at[:cut], key_tail), (low_values, high_values))):
        head_count, group, width = weight.shape
        for block in blocks:
            groups = block.shape[0] // group
            for head in range(head_count):
                lanes = slice(head * width, (head + 1) * width)
                grouped = block[:, lanes].astype(jnp.float32).reshape(groups, group, width)
                summed = jnp.sum(grouped * weight[head].astype(jnp.float32)[None], axis=1)
                lead[row : row + groups, lanes] = summed.astype(lead.dtype)
            row += groups


def prepare(keys, values, key_weight, value_weight, cut, half):
    rows, channels = keys.shape
    groups = rows // key_weight.shape[1]
    shapes = [(cut + 2 * groups, channels), (rows - cut, channels), (half, channels), (rows - half, channels)]
    return pl.pallas_call(
        prepare_kernel,
        name="prepare",
        out_shape=[jax.ShapeDtypeStruct(shape, keys.dtype) for shape in shapes],
        in_specs=[pl.BlockSpec(memory_space=pltpu.HBM)] * 4,
        out_specs=[vmem_spec] * 4,
        scratch_shapes=[
            pltpu.VMEM(key_weight.shape, key_weight.dtype),
            pltpu.VMEM(value_weight.shape, value_weight.dtype),
            pltpu.SemaphoreType.DMA((6,)),
        ],
        compiler_params=pltpu.CompilerParams(vmem_limit_bytes=16 << 20),
        cost_estimate=pl.CostEstimate(flops=4 * rows * channels, bytes_accessed=4 * rows * channels, transcendentals=0),
    )(keys, values, key_weight, value_weight)


def attend_kernel(layout, first, last, width, *refs):
    queries, rest = refs[0], list(refs[1:])
    sets = []
    for count in layout:
        if isinstance(count, int):
            sets.append(([r.at[0] for r in rest[:count]], [r.at[1] for r in rest[:count]]))
            rest = rest[count:]
        else:
            keys_in, values_in = count
            taken = [r.at[:n] for r, n in zip(rest, keys_in + values_in)]
            sets.append((taken[: len(keys_in)], taken[len(keys_in) :]))
            rest = rest[len(taken) :]
    if not first:
        top_in, total_in, sum_in, rest = *rest[:3], rest[3:]
    heads = queries.shape[1] // width
    factor = math.log2(math.e) / math.sqrt(width)
    for head in range(heads):
        lanes = slice(head * width, (head + 1) * width)
        join = lambda blocks: jnp.concatenate([b[:, lanes] for b in blocks], 0) if len(blocks) > 1 else blocks[0][:, lanes]
        query = queries[:, lanes]
        scores = [
            lax.dot_general(query, join(k), (((1,), (1,)), ((), ())), preferred_element_type=jnp.float32)
            for k, _ in sets
        ]
        top = functools.reduce(jnp.maximum, [jnp.max(s, axis=1, keepdims=True) for s in scores])
        if not first:
            top_before = top_in[:, lanes][:, :1]
            top = jnp.maximum(top, top_before)
        weights = [jnp.exp2((s - top) * factor) for s in scores]
        total = sum(jnp.sum(w, axis=1, keepdims=True) for w in weights)
        summed = sum(
            jnp.dot(w.astype(jnp.bfloat16), join(v), preferred_element_type=jnp.float32)
            for w, (_, v) in zip(weights, sets)
        )
        if not first:
            decay = jnp.exp2((top_before - top) * factor)
            total = total + decay * total_in[:, lanes][:, :1]
            summed = summed + decay * sum_in[:, lanes]
        if last:
            rest[0][:, lanes] = (summed * (1.0 / total)).astype(jnp.bfloat16)
        else:
            rest[0][:, lanes] = jnp.broadcast_to(top, summed.shape)
            rest[1][:, lanes] = jnp.broadcast_to(total, summed.shape)
            rest[2][:, lanes] = summed


def attend(carried, queries, sets, width, last=False):
    rows, channels = queries.shape
    layout, operands, key_count = [], [queries], 0
    for entry in sets:
        if isinstance(entry, tuple):
            layout.append(tuple([n for _, n in blocks] for blocks in entry))
            operands += [x for blocks in entry for x, _ in blocks]
            key_count += sum(layout[-1][0])
        else:
            layout.append(len(entry))
            operands += entry
            key_count += sum(k.shape[1] for k in entry)
    operands += carried or ()
    if last:
        out_shape = jax.ShapeDtypeStruct((rows, channels), jnp.bfloat16)
        out_specs = vmem_spec
    else:
        out_shape = [jax.ShapeDtypeStruct((rows, channels), jnp.float32)] * 3
        out_specs = [vmem_spec] * 3
    return pl.pallas_call(
        functools.partial(attend_kernel, layout, carried is None, last, width),
        name="attend",
        out_shape=out_shape,
        in_specs=[vmem_spec] * len(operands),
        out_specs=out_specs,
        compiler_params=pltpu.CompilerParams(vmem_limit_bytes=24 << 20),
        cost_estimate=pl.CostEstimate(
            flops=8 * rows * key_count * channels,
            bytes_accessed=4 * key_count * channels + 4 * rows * channels,
            transcendentals=rows * key_count * channels // width,
        ),
    )(*operands)


def move(rows, pairs):
    return lax.ppermute(rows, "ctx", pairs)


def body(queries, keys, values, key_weight, value_weight):
    width = key_weight.shape[2]
    size = lax.axis_size("ctx")
    block, channels = keys.shape
    cut, half, groups = key_cut, value_cut, block // key_weight.shape[1]
    core, y_side, z_one, z_two = (bit_perm(size, bit) for bit in range(4))
    z_side = z_perm(size, lambda z: z + 2 if z & 2 else z - 2)
    z_odd = z_perm(size, lambda z: z + 1 if z & 1 else z - 1)

    lead, key_tail, low_values, high_values = prepare(keys, values, key_weight, value_weight, cut, half)
    own_rows = lead[cut:]
    two = [move(lead, z_two), move(low_values, z_two), move(key_tail, z_two), move(high_values, z_two)]
    four = [move(jnp.concatenate([two[0], own_rows], 0), z_side)]
    four += [move(two[i], z_side) for i in range(1, 4)]
    one = move(keys, z_one), move(values, z_one)
    twin = move(keys, core), move(values, core)
    side = move(keys, y_side), move(values, y_side)

    stacked = [x.reshape(2, groups, channels) for x in (own_rows, two[0][cut:], four[0][cut : cut + 2 * groups], four[0][cut + 2 * groups :])]
    even = jnp.concatenate(stacked, 1)
    odd = move(even, z_odd)
    even_side, odd_side = move(even, y_side), move(odd, y_side)
    comp_even = [even, even_side, move(even, core), move(even_side, core)]
    comp_odd = [odd, odd_side, move(odd, core), move(odd_side, core)]

    whole = lambda *blocks: [(x, block) for x in blocks]
    parts = lambda c: ([(c[0], cut), (c[2], block - cut)], [(c[1], half), (c[3], block - half)])
    stages = {
        "own": [parts((lead, low_values, key_tail, high_values)), (whole(twin[0]), whole(twin[1]))],
        "side": [(whole(side[0]), whole(side[1]))],
        "even": [comp_even],
        "odd": [comp_odd, parts(two)],
        "one": [(whole(one[0]), whole(one[1]))],
        "rest": [parts(four)],
    }
    carried = None
    for name, sets in stages.items():
        carried = attend(carried, queries, sets, width, last=name == "rest")
    return lax.all_to_all(carried, "head", split_axis=0, concat_axis=1, tiled=True)


key_cut = 128
value_cut = 384


def solution(mesh):
    in_specs = (
        P("ctx", "head"),
        P("ctx", "head"),
        P("ctx", "head"),
        P("head", None, None),
        P("head", None, None),
    )
    out_specs = P(("ctx", "head"), None)

    return jax.shard_map(body, mesh=mesh, in_specs=in_specs, out_specs=out_specs, check_vma=False)
```

```python
import functools
import math

import jax
import jax.numpy as jnp
from jax import lax
from jax.experimental import pallas as pl
from jax.experimental.pallas import tpu as pltpu
from jax.sharding import PartitionSpec as P


vmem_spec = pl.BlockSpec(memory_space=pltpu.VMEM)


def z_perm(size, target):
    return [(i, target(i // 4) % (size // 4) * 4 + i % 4) for i in range(size)]


def bit_perm(size, bit):
    return [(i, i ^ (1 << bit)) for i in range(size)]


def prepare_kernel(keys, values, key_weight, value_weight, lead, key_tail, low_values, high_values, *scratch):
    weights, sems = scratch[:2], scratch[2]
    cut, half = keys.shape[0] - key_tail.shape[0], low_values.shape[0]
    copies = [
        pltpu.make_async_copy(source, target, sems.at[index])
        for index, (source, target) in enumerate(
            (
                (key_weight, weights[0]),
                (keys.at[:cut], lead.at[:cut]),
                (keys.at[cut:], key_tail),
                (value_weight, weights[1]),
                (values.at[:half], low_values),
                (values.at[half:], high_values),
            )
        )
    ]
    for copy in copies:
        copy.start()
    row = cut
    for side, blocks in enumerate(((lead.at[:cut], key_tail), (low_values, high_values))):
        for copy in copies[3 * side : 3 * side + 3]:
            copy.wait()
        weight = weights[side]
        head_count, group, width = weight.shape
        for block in blocks:
            groups = block.shape[0] // group
            for head in range(head_count):
                lanes = slice(head * width, (head + 1) * width)
                grouped = block[:, lanes].astype(jnp.float32).reshape(groups, group, width)
                summed = jnp.sum(grouped * weight[head].astype(jnp.float32)[None], axis=1)
                lead[row : row + groups, lanes] = summed.astype(lead.dtype)
            row += groups


def prepare(keys, values, key_weight, value_weight, cut, half):
    rows, channels = keys.shape
    groups = rows // key_weight.shape[1]
    shapes = [(cut + 2 * groups, channels), (rows - cut, channels), (half, channels), (rows - half, channels)]
    return pl.pallas_call(
        prepare_kernel,
        name="prepare",
        out_shape=[jax.ShapeDtypeStruct(shape, keys.dtype) for shape in shapes],
        in_specs=[pl.BlockSpec(memory_space=pltpu.HBM)] * 4,
        out_specs=[vmem_spec] * 4,
        scratch_shapes=[
            pltpu.VMEM(key_weight.shape, key_weight.dtype),
            pltpu.VMEM(value_weight.shape, value_weight.dtype),
            pltpu.SemaphoreType.DMA((6,)),
        ],
        compiler_params=pltpu.CompilerParams(vmem_limit_bytes=16 << 20),
        cost_estimate=pl.CostEstimate(flops=4 * rows * channels, bytes_accessed=4 * rows * channels, transcendentals=0),
    )(keys, values, *(pltpu.with_memory_space_constraint(w, pltpu.HBM) for w in (key_weight, value_weight)))


def attend_kernel(layout, first, last, width, *refs):
    queries, rest = refs[0], list(refs[1:])
    sets = []
    for count in layout:
        if isinstance(count, int):
            sets.append(([r.at[0] for r in rest[:count]], [r.at[1] for r in rest[:count]]))
            rest = rest[count:]
        else:
            keys_in, values_in = count
            taken = [r.at[:n] for r, n in zip(rest, keys_in + values_in)]
            sets.append((taken[: len(keys_in)], taken[len(keys_in) :]))
            rest = rest[len(taken) :]
    if not first:
        top_in, total_in, sum_in, rest = *rest[:3], rest[3:]
    heads = queries.shape[1] // width
    factor = math.log2(math.e) / math.sqrt(width)
    for head in range(heads):
        lanes = slice(head * width, (head + 1) * width)
        join = lambda blocks: jnp.concatenate([b[:, lanes] for b in blocks], 0) if len(blocks) > 1 else blocks[0][:, lanes]
        query = queries[:, lanes]
        scores = [
            lax.dot_general(query, join(k), (((1,), (1,)), ((), ())), preferred_element_type=jnp.float32)
            for k, _ in sets
        ]
        top = functools.reduce(jnp.maximum, [jnp.max(s, axis=1, keepdims=True) for s in scores])
        if not first:
            top_before = top_in[:, lanes][:, :1]
            top = jnp.maximum(top, top_before)
        weights = [jnp.exp2((s - top) * factor) for s in scores]
        total = sum(jnp.sum(w, axis=1, keepdims=True) for w in weights)
        summed = sum(
            jnp.dot(w.astype(jnp.bfloat16), join(v), preferred_element_type=jnp.float32)
            for w, (_, v) in zip(weights, sets)
        )
        if not first:
            decay = jnp.exp2((top_before - top) * factor)
            total = total + decay * total_in[:, lanes][:, :1]
            summed = summed + decay * sum_in[:, lanes]
        if last:
            rest[0][:, lanes] = (summed * (1.0 / total)).astype(jnp.bfloat16)
        else:
            rest[0][:, lanes] = jnp.broadcast_to(top, summed.shape)
            rest[1][:, lanes] = jnp.broadcast_to(total, summed.shape)
            rest[2][:, lanes] = summed


def attend(carried, queries, sets, width, last=False):
    rows, channels = queries.shape
    layout, operands, key_count = [], [queries], 0
    for entry in sets:
        if isinstance(entry, tuple):
            layout.append(tuple([n for _, n in blocks] for blocks in entry))
            operands += [x for blocks in entry for x, _ in blocks]
            key_count += sum(layout[-1][0])
        else:
            layout.append(len(entry))
            operands += entry
            key_count += sum(k.shape[1] for k in entry)
    operands += carried or ()
    if last:
        out_shape = jax.ShapeDtypeStruct((rows, channels), jnp.bfloat16)
        out_specs = vmem_spec
    else:
        out_shape = [jax.ShapeDtypeStruct((rows, channels), jnp.float32)] * 3
        out_specs = [vmem_spec] * 3
    return pl.pallas_call(
        functools.partial(attend_kernel, layout, carried is None, last, width),
        name="attend",
        out_shape=out_shape,
        in_specs=[vmem_spec] * len(operands),
        out_specs=out_specs,
        compiler_params=pltpu.CompilerParams(vmem_limit_bytes=24 << 20),
        cost_estimate=pl.CostEstimate(
            flops=8 * rows * key_count * channels,
            bytes_accessed=4 * key_count * channels + 4 * rows * channels,
            transcendentals=rows * key_count * channels // width,
        ),
    )(*operands)


def move(rows, pairs):
    return lax.ppermute(rows, "ctx", pairs)


def body(queries, keys, values, key_weight, value_weight):
    width = key_weight.shape[2]
    size = lax.axis_size("ctx")
    block, channels = keys.shape
    cut, half, groups = key_cut, value_cut, block // key_weight.shape[1]
    core, y_side, z_one, z_two = (bit_perm(size, bit) for bit in range(4))
    z_side = z_perm(size, lambda z: z + 2 if z & 2 else z - 2)
    z_odd = z_perm(size, lambda z: z + 1 if z & 1 else z - 1)

    lead, key_tail, low_values, high_values = prepare(keys, values, key_weight, value_weight, cut, half)
    own_rows = lead[cut:]
    two = [move(lead, z_two), move(low_values, z_two), move(key_tail, z_two), move(high_values, z_two)]
    four = [move(jnp.concatenate([two[0], own_rows], 0), z_side)]
    four += [move(two[i], z_side) for i in range(1, 4)]
    one = move(keys, z_one), move(values, z_one)
    twin = move(keys, core), move(values, core)
    side = move(keys, y_side), move(values, y_side)

    stacked = [x.reshape(2, groups, channels) for x in (own_rows, two[0][cut:], four[0][cut : cut + 2 * groups], four[0][cut + 2 * groups :])]
    even = jnp.concatenate(stacked, 1)
    odd = move(even, z_odd)
    even_side, odd_side = move(even, y_side), move(odd, y_side)
    comp_even = [even, even_side, move(even, core), move(even_side, core)]
    comp_odd = [odd, odd_side, move(odd, core), move(odd_side, core)]

    whole = lambda *blocks: [(x, block) for x in blocks]
    parts = lambda c: ([(c[0], cut), (c[2], block - cut)], [(c[1], half), (c[3], block - half)])
    stages = {
        "own": [parts((lead, low_values, key_tail, high_values)), (whole(twin[0]), whole(twin[1]))],
        "side": [(whole(side[0]), whole(side[1]))],
        "even": [comp_even],
        "odd": [comp_odd, parts(two)],
        "one": [(whole(one[0]), whole(one[1]))],
        "rest": [parts(four)],
    }
    carried = None
    for name, sets in stages.items():
        carried = attend(carried, queries, sets, width, last=name == "rest")
    return lax.all_to_all(carried, "head", split_axis=0, concat_axis=1, tiled=True)


key_cut = 128
value_cut = 384


def solution(mesh):
    in_specs = (
        P("ctx", "head"),
        P("ctx", "head"),
        P("ctx", "head"),
        P("head", None, None),
        P("head", None, None),
    )
    out_specs = P(("ctx", "head"), None)

    return jax.shard_map(body, mesh=mesh, in_specs=in_specs, out_specs=out_specs, check_vma=False)
```
